32 devices in a mesh: row: 4 (over z), bulk: 8 (over y, x, core).
Axes of the slice: x: 2, y: 2, z: 4, core: 2. Of those that a mesh axis runs over, the one named last changes fastest.
Arguments:
- child_inverse: float32 [2, 4096, 4096], P(None, 'row', 'bulk')
- child_rhs: float32 [2, 4096, 256], P(None, 'bulk'), may hold values from -6 to 6
- child_update: float32 [2, 1024, 4096], P(None, 'bulk', 'row'), may hold values from -0.09375 to 0.09375
- targets: int32 [2, 1024], replicated, may hold values from 0 to 8191, as said below
- root_inverse: float32 [8192, 8192], P('row', 'bulk')
- root_rhs: float32 [8192, 256], P('bulk'), may hold values from -6 to 6
Outputs:
- root_solution: float32 [8192, 256], P('bulk')
- child_solution: float32 [2, 4096, 256], P(None, 'bulk')
The draws below stay inside these ranges and needn't reach their ends.
Inputs may be any that keep to these rules, and one draw needn't show every extreme that they name: `targets`: for each child, the 128 update rows k * 128 to (k + 1) * 128 - 1 name at most 32 rows of one owner, the owner of root row t being t // 1024; in every such block some owner is named exactly 32 times. A root row may be named more than once.
All inputs are finite; a program needn't handle non-finite values.
Results may differ from the reference program's by a relative error of at most 0.00007.
Values sent between devices are 32-bit elements; how exact they have to be, the bound alone decides.
A program may use at most 128 MiB of HBM per device.

```python
import math
import jax
import jax.numpy as jnp
from jax import lax

WC = 4096
WR = 8192
R = 256
NL = 128
NU = 1024
RB = 1024
CAP = 32


def lower_inverse(key, width, lead):
    key_off, key_diag = jax.random.split(key)
    positions = jnp.arange(width)
    ordering = positions % 32 * (width // 32) + positions // 32
    below = ordering[:, None] > ordering[None, :]
    diagonal = ordering[:, None] == ordering[None, :]
    spread = jax.random.normal(key_off, lead + (width, width), jnp.float32)
    entries = spread * (0.7 / math.sqrt(width))
    diag_values = jax.random.uniform(key_diag, lead + (width, width), jnp.float32, 0.6, 1.4)
    return jnp.where(below, entries, 0.0) + jnp.where(diagonal, diag_values, 0.0)


def draw_child_inverse(key, part):
    return lower_inverse(jax.random.fold_in(key, 11), WC, (2,)).astype(jnp.float32)


def draw_root_inverse(key, part):
    return lower_inverse(jax.random.fold_in(key, 23), WR, ()).astype(jnp.float32)


def draw_targets(key, part):
    keys = jax.random.split(jax.random.fold_in(key, 37), 4)
    sources = NU // NL
    owners = WR // RB
    slots = owners * CAP
    hot_owner = jax.random.randint(keys[0], (2, sources), 0, owners)
    slot_owner = jnp.arange(slots) // CAP
    scores = jax.random.randint(keys[1], (2, sources, slots), 0, 1048576) * slots + jnp.arange(slots)[None, None, :]
    scores = jnp.where(slot_owner[None, None, :] == hot_owner[:, :, None], jnp.arange(slots)[None, None, :] - slots, scores)
    chosen = jnp.argsort(scores, axis=2, stable=True)[:, :, :NL]
    chosen_owner = chosen // CAP
    order = jax.random.randint(keys[2], (2, sources, NL), 0, 1048576) * NL + jnp.arange(NL)[None, None, :]
    shuffle = jnp.argsort(order, axis=2, stable=True)
    owner_of = jnp.take_along_axis(chosen_owner, shuffle, axis=2)
    within = jax.random.randint(keys[3], (2, sources, NL), 0, RB)
    return (owner_of * RB + within).reshape(2, NU).astype(jnp.int32)


def steps_of(rng, shape, pieces, least, high):
    gain, own = 1.0, jax.random.fold_in(rng, 6)
    for position, parts in pieces:
        steps = jnp.exp(jax.random.uniform(jax.random.fold_in(own, position), (parts,), jnp.float32, least / len(pieces), high / len(pieces)))
        gain = gain * jnp.repeat(steps, shape[position] // parts).reshape([-1 if axis == position else 1 for axis in range(len(shape))])
    return gain


def normal_values(rng, dims, scale, most, shards=(), dtype=jnp.bfloat16):
    drawn = jax.random.normal(rng, dims, jnp.float32) * scale
    if len(shards) > 0:
        drawn = steps_of(rng, dims, shards, -0.22, 0.18) * drawn
    return jnp.clip(drawn, min=-most, max=most).astype(dtype)


def setup_inputs(seed: int = 0) -> dict:
    key_of = jax.random.split(jax.random.key(seed), 7)
    return {
        "child_inverse": draw_child_inverse(jax.random.fold_in(key_of[6], 71), 0),
        "child_rhs": normal_values(key_of[1], (2, WC, R), 1.0, 6.0, ((1, 8),), jnp.float32),
        "child_update": normal_values(key_of[2], (2, NU, WC), WC ** -0.5, 0.09375, ((1, 8), (2, 4)), jnp.float32),
        "targets": draw_targets(jax.random.fold_in(key_of[6], 71), 0),
        "root_inverse": draw_root_inverse(jax.random.fold_in(key_of[6], 71), 0),
        "root_rhs": normal_values(key_of[5], (WR, R), 1.0, 6.0, ((0, 8),), jnp.float32),
    }


def reference(child_inverse, child_rhs, child_update, targets, root_inverse, root_rhs):
    highest = lax.Precision.HIGHEST
    forward_child = jnp.einsum('jab,jbr->jar', child_inverse, child_rhs, precision=highest)
    update = jnp.einsum('jua,jar->jur', child_update, forward_child, precision=highest)
    assembled = jnp.zeros((WR, R), jnp.float32).at[targets.reshape(-1)].add(update.reshape(-1, R))
    forward_root = jnp.dot(root_inverse, root_rhs - assembled, precision=highest)
    root_solution = jnp.dot(root_inverse.T, forward_root, precision=highest)
    fetched = root_solution[targets]
    coupling = jnp.einsum('jua,jur->jar', child_update, fetched, precision=highest)
    child_solution = jnp.einsum('jab,jar->jbr', child_inverse, forward_child - coupling, precision=highest)
    return root_solution, child_solution
```

```python
import functools

import jax
import jax.numpy as jnp
from jax import lax
from jax.experimental import pallas as pl
from jax.experimental.pallas import tpu as pltpu
from jax.sharding import PartitionSpec as P

MESH = pl.DeviceIdType.MESH
CHUNKS = 2
OFFSET = 3
f32, bf16 = jnp.float32, jnp.bfloat16


def split(x):
    high = x.astype(bf16)
    return high, (x - high.astype(f32)).astype(bf16)


def bit_orders(bits):
    rest = list(range(1, bits))
    return ([0] + rest, [0] + rest[::-1])


def block_position(block, order, bits):
    position = 0
    for step, bit in enumerate(order):
        position += ((block >> bit) & 1) << (bits - 1 - step)
    return position


def dot(a, b):
    return jnp.dot(a, b, preferred_element_type=f32)


def kernel(
    nb, nr, dims,
    ci_hbm, crhs_ref, cu_hbm, trow_ref, tcol_ref, ri_hbm, rrhs_ref,
    root_out, child_out,
    ci, cu, ri,
    part, fcr, fc, ug, frp, frr, fr, rep, repr_, cp, cpr,
    up, upx, bk, bkx, cb, cbx,
    rhs_w, tmp_t,
    load_sem, ar_s, ar_r, ch_s, ch_r,
):
    bits = nb.bit_length() - 1
    orders = bit_orders(bits)
    me = lax.axis_index("bulk")
    row = lax.axis_index("row")
    C = fc.shape[-1]
    cols_a, cols_b, own, rows_a, nl = dims

    loads = [
        pltpu.make_async_copy(ci_hbm, ci, load_sem.at[0]),
        pltpu.make_async_copy(cu_hbm, cu, load_sem.at[1]),
        pltpu.make_async_copy(ri_hbm, ri, load_sem.at[2]),
    ]
    for load in loads:
        load.start()

    def partner_of(bit):
        size = 1 << bit
        mine = (me // size) % 2
        return mine, me + size * (1 - 2 * mine)

    right = lax.rem(row + 1, nr)
    left = lax.rem(row + nr - 1, nr)
    barrier = pltpu.get_barrier_semaphore()
    for bit in range(bits):
        pl.semaphore_signal(barrier, inc=1, device_id={"bulk": partner_of(bit)[1]}, device_id_type=MESH)

    for side in (left, right):
        pl.semaphore_signal(barrier, inc=1, device_id={"row": side}, device_id_type=MESH)
    pl.semaphore_wait(barrier, bits + 2)

    def remote(src, dst, send, recv, **where):
        return pltpu.make_async_remote_copy(
            src_ref=src, dst_ref=dst, send_sem=send, recv_sem=recv, device_id=where, device_id_type=MESH
        )

    def reduce_scatter(h, which, buf, rbuf, starts, out):
        n = buf.shape[2]
        length, off, sends = n, 0, []
        for step in range(bits):
            half = length // 2
            flights = []
            for f in range(2):
                mine, partner = partner_of(orders[f][step])
                away = pl.multiple_of(starts[f] + (1 - mine) * half, half)
                keep = pl.multiple_of(starts[f] + mine * half, half)
                copy = remote(
                    buf.at[h, f, pl.ds(away, half)], rbuf.at[h, f, pl.ds(off, half)],
                    ar_s.at[h, which, f, step], ar_r.at[h, which, f, step], bulk=partner,
                )
                copy.start()
                flights.append((copy, keep))
            yield
            for f, (copy, keep) in enumerate(flights):
                copy.wait_recv()
                target = out if step == bits - 1 else buf
                target[h, f, pl.ds(keep, half)] = buf[h, f, pl.ds(keep, half)] + rbuf[h, f, pl.ds(off, half)]
                starts[f] = keep
                sends.append(copy)
            length, off = half, off + half
        for copy in sends:
            copy.wait_send()

    def all_gather(h, which, buf, starts):
        n = buf.shape[2]
        for step in reversed(range(bits)):
            length = n >> (step + 1)
            flights = []
            for f in range(2):
                mine, partner = partner_of(orders[f][step])
                here = buf.at[h, f, pl.ds(pl.multiple_of(starts[f], length), length)]
                copy = remote(
                    here, here, ar_s.at[h, which, f, step], ar_r.at[h, which, f, step], bulk=partner
                )
                copy.start()
                flights.append((copy, mine))
            yield
            for f, (copy, mine) in enumerate(flights):
                copy.wait_send()
                copy.wait_recv()
                starts[f] = starts[f] - mine * length

    def chain(h, which, p, x):
        pieces = p.shape[1]

        @pl.when(row == 0)
        def _():
            x[h, 0] = jnp.zeros(x.shape[2:], f32)

        @pl.when(row == nr - 1)
        def _():
            x[h, 1] = jnp.zeros(x.shape[2:], f32)

        def flow(side, i, has_source, has_target, target):
            copy = remote(
                x.at[h, 2 + side, i], x.at[h, side, i],
                ch_s.at[h, which, side, i], ch_r.at[h, which, side, i], row=target,
            )

            @pl.when(has_source)
            def _():
                copy.wait_recv()

            @pl.when(has_target)
            def _():
                x[h, 2 + side, i] = x[h, side, i] + p[h, i]
                copy.start()

        for t in range(pieces + nr - 1):
            if t > 0:
                yield
            i = t - row

            @pl.when((i >= 0) & (i < pieces))
            def _():
                flow(0, i, row > 0, row < nr - 1, right)

            k = t - (nr - 1 - row)

            @pl.when((k >= 0) & (k < pieces))
            def _():
                flow(1, k, row < nr - 1, row > 0, left)

        for i in range(pieces):
            for side, has_target, target in ((0, row < nr - 1, right), (1, row > 0, left)):
                @pl.when(has_target)
                def _():
                    remote(
                        x.at[h, 2 + side, i], x.at[h, side, i],
                        ch_s.at[h, which, side, i], ch_r.at[h, which, side, i], row=target,
                    ).wait_send()

    def times(a_tile, count, store, h, width):
        def body(i, carry):
            high, low = split(a_tile(i))
            both = dot(high, rhs_w[h, :width]) + dot(low, rhs_w[h, :width])
            store(i, both[:, :C] + both[:, C:])
            return carry

        lax.fori_loop(0, count, body, 0)

    def keep_right(h, at, value):
        high, low = split(value)
        rhs_w[h, at, :C] = high
        rhs_w[h, at, C:] = low

    def transposed_times(a_tile, depth, k_tile, y_tile, count, width, store, h):
        for k in range(depth // k_tile):
            high, low = split(y_tile(k).T)
            tmp_t[h, :C, k * k_tile:(k + 1) * k_tile] = high
            tmp_t[h, C:, k * k_tile:(k + 1) * k_tile] = low

        def body(i, carry):
            total = jnp.zeros((2 * C, width), f32)
            for k in range(depth // k_tile):
                high, low = split(a_tile(k, i))
                y = tmp_t[h, :, k * k_tile:(k + 1) * k_tile]
                total += dot(y, high) + dot(y, low)
            store(i, (total[:C] + total[C:]).T)
            return carry

        lax.fori_loop(0, count, body, 0)

    def tiles(n, most):
        size = min(n, most)
        return size, n // size

    def program(h):
        lanes = slice(h * C, (h + 1) * C)
        if h == 0:
            loads[0].wait()
        tm, count = tiles(cols_a, 256)
        for j in range(2):
            keep_right(h, slice(0, cols_b), crhs_ref[j, :, lanes])

            def store(i, value, j=j):
                part[h, j, pl.ds(pl.multiple_of(i * tm, tm), tm)] = value

            times(lambda i, j=j: ci[j, pl.ds(pl.multiple_of(i * tm, tm), tm), :], count, store, h, cols_b)
        starts = [0, 0]
        yield from reduce_scatter(h, 0, part, fcr, starts, fc)
        yield from all_gather(h, 1, fc, starts)
        if h == 0:
            loads[1].wait()
        for j in range(2):
            keep_right(h, slice(0, cols_a), fc[h, j])

            def store(i, value, j=j):
                up[h, j] = value

            times(lambda i, j=j: cu[j], 1, store, h, cols_a)
        yield from chain(h, 0, up, upx)
        starts = []
        for j in range(2):
            position = 0
            for step, bit in enumerate(orders[j]):
                position = position + ((me // (1 << bit)) % 2) * (1 << (bits - 1 - step))
            start = pl.multiple_of(position * nl, nl)
            starts.append(start)
            ug[h, j, pl.ds(start, nl)] = upx[h, 0, j] + up[h, j] + upx[h, 1, j]
        yield from all_gather(h, 2, ug, starts)
        tm, count = tiles(own, 256)
        nu = nb * nl
        kt, kcount = tiles(nu, 512)

        def assemble(i, carry):
            ids = lax.broadcasted_iota(jnp.int32, (tm, kt), 0) + (me * own + i * tm)
            at = pl.ds(pl.multiple_of(i * tm, tm), tm)
            total = jnp.zeros((tm, C), f32)
            for j in range(2):
                for k in range(kcount):
                    ks = slice(k * kt, (k + 1) * kt)
                    hit = jnp.where(ids == trow_ref[j:j + 1, ks], 1.0, 0.0).astype(bf16)
                    high, low = split(ug[h, j, ks])
                    total += dot(hit, high) + dot(hit, low)
            value = rrhs_ref[at, lanes] - total
            high, low = split(value)
            rhs_w[h, at, :C] = high
            rhs_w[h, at, C:] = low
            return carry

        lax.fori_loop(0, count, assemble, 0)
        if h == 0:
            loads[2].wait()
        per = rows_a // 2
        tm4, count4 = tiles(per, 256)
        for f in range(2):
            def store(i, value, f=f):
                frp[h, f, pl.ds(pl.multiple_of(i * tm4, tm4), tm4)] = value

            times(
                lambda i, f=f: ri[pl.ds(pl.multiple_of(f * per + i * tm4, tm4), tm4), :],
                count4, store, h, own,
            )
        starts = [0, 0]
        yield from reduce_scatter(h, 3, frp, frr, starts, fr)
        yield from all_gather(h, 4, fr, starts)
        pieces, size = bk.shape[1], bk.shape[2]
        width = min(256, own)
        kt5, _ = tiles(per, 512)
        halves = per // kt5

        def store(i, value):
            for s in range(max(1, width // size)):
                piece = min(width, size)
                if size >= width:
                    each = size // width
                    bk[h, i // each, pl.ds(pl.multiple_of((i % each) * width, width), width)] = value
                else:
                    bk[h, i * (width // size) + s] = value[s * piece:(s + 1) * piece]

        transposed_times(
            lambda k, i: ri[k * kt5:(k + 1) * kt5, pl.ds(pl.multiple_of(i * width, width), width)],
            rows_a, kt5,
            lambda k: fr[h, k // halves, (k % halves) * kt5:(k % halves + 1) * kt5],
            own // width, width, store, h,
        )
        yield from chain(h, 1, bk, bkx)
        for i in range(pieces):
            value = bkx[h, 0, i] + bk[h, i] + bkx[h, 1, i]
            root_out[i * size:(i + 1) * size, lanes] = value
            keep_right(h, slice(i * size, (i + 1) * size), value)
        tm6, count6 = tiles(nu, 256)
        for j in range(2):
            def fetch(i, carry, j=j):
                at = pl.ds(pl.multiple_of(i * tm6, tm6), tm6)
                ids = lax.broadcasted_iota(jnp.int32, (tm6, own), 1) + me * own
                hit = jnp.where(ids == tcol_ref[j, at], 1.0, 0.0).astype(bf16)
                both = dot(hit, rhs_w[h, :own])
                rep[h, j, at] = both[:, :C] + both[:, C:]
                return carry

            lax.fori_loop(0, count6, fetch, 0)
        starts = [0, 0]
        yield from reduce_scatter(h, 5, rep, repr_, starts, rep)
        w7, count7 = tiles(cols_a, 256)
        for j in range(2):
            def store(i, value, j=j):
                cp[h, j, pl.ds(pl.multiple_of(i * w7, w7), w7)] = value

            transposed_times(
                lambda k, i, j=j: cu[j, :, pl.ds(pl.multiple_of(i * w7, w7), w7)],
                nl, nl,
                lambda k, j=j: rep[h, j, pl.ds(starts[j], nl)],
                count7, w7, store, h,
            )
        starts7 = [0, 0]
        yield from reduce_scatter(h, 6, cp, cpr, starts7, part)
        yield from all_gather(h, 7, part, starts7)
        pieces8, size8 = cb.shape[1], cb.shape[2]
        w8, count8 = tiles(cols_b, size8)
        kt8, _ = tiles(cols_a, 512)
        for j in range(2):
            def store(i, value, j=j):
                cb[h, j * (pieces8 // 2) + i] = value

            transposed_times(
                lambda k, i, j=j: ci[j, k * kt8:(k + 1) * kt8, pl.ds(pl.multiple_of(i * w8, w8), w8)],
                cols_a, kt8,
                lambda k, j=j: fc[h, j, k * kt8:(k + 1) * kt8] - part[h, j, k * kt8:(k + 1) * kt8],
                count8, w8, store, h,
            )
        yield from chain(h, 2, cb, cbx)
        for i in range(pieces8):
            j, k = i // (pieces8 // 2), i % (pieces8 // 2)
            child_out[j, k * size8:(k + 1) * size8, lanes] = cbx[h, 0, i] + cb[h, i] + cbx[h, 1, i]

    running = [program(h) for h in range(CHUNKS)]
    turn = 0
    while any(p is not None for p in running):
        for h in range(CHUNKS):
            if running[h] is not None and turn >= h * OFFSET:
                try:
                    next(running[h])
                except StopIteration:
                    running[h] = None
        turn += 1


def per_device(nb, nr, child_inverse, child_rhs, child_update, targets, root_inverse, root_rhs):
    bits = nb.bit_length() - 1
    orders = bit_orders(bits)
    _, cols_a, cols_b = child_inverse.shape
    nl = child_update.shape[1]
    rows_a, own = root_inverse.shape
    R = root_rhs.shape[1]
    H, C = CHUNKS, R // CHUNKS
    nu = nb * nl
    blocks = targets.reshape(2, nb, nl)
    placed = []
    for j in range(2):
        source = [0] * nb
        for block in range(nb):
            source[block_position(block, orders[j], bits)] = block
        placed.append(jnp.concatenate([blocks[j, s] for s in source]))
    trow = jnp.stack(placed)
    tcol = trow[:, :, None]
    root_pieces = max(1, min(4, own // 128))
    child_pieces = 2 * max(1, min(2, cols_b // 128))
    most = max(root_pieces, child_pieces, 2)
    any_, vmem = pl.BlockSpec(memory_space=pl.ANY), pl.BlockSpec(memory_space=pltpu.VMEM)

    def sums(n, count=2):
        return [pltpu.VMEM((H, 2, n, C), f32)] * count

    def chains(pieces, rows):
        return [pltpu.VMEM((H, pieces, rows, C), f32), pltpu.VMEM((H, 4, pieces, rows, C), f32)]

    return pl.pallas_call(
        functools.partial(kernel, nb, nr, (cols_a, cols_b, own, rows_a, nl)),
        out_shape=(
            jax.ShapeDtypeStruct(root_rhs.shape, f32),
            jax.ShapeDtypeStruct(child_rhs.shape, f32),
        ),
        in_specs=[any_, vmem, any_, vmem, vmem, any_, vmem],
        out_specs=(vmem, vmem),
        scratch_shapes=[
            pltpu.VMEM(child_inverse.shape, f32),
            pltpu.VMEM(child_update.shape, f32),
            pltpu.VMEM(root_inverse.shape, f32),
            *sums(cols_a, 3),
            pltpu.VMEM((H, 2, nu, C), f32),
            *sums(rows_a // 2, 3),
            *sums(nu),
            *sums(cols_a),
            *chains(2, nl),
            *chains(root_pieces, own // root_pieces),
            *chains(child_pieces, 2 * cols_b // child_pieces),
            pltpu.VMEM((H, max(own, cols_a, cols_b), 2 * C), bf16),
            pltpu.VMEM((H, 2 * C, max(rows_a, cols_a, nl)), bf16),
            pltpu.SemaphoreType.DMA((3,)),
            pltpu.SemaphoreType.DMA((H, 8, 2, bits)),
            pltpu.SemaphoreType.DMA((H, 8, 2, bits)),
            pltpu.SemaphoreType.DMA((H, 3, 2, most)),
            pltpu.SemaphoreType.DMA((H, 3, 2, most)),
        ],
        compiler_params=pltpu.CompilerParams(
            collective_id=0, has_side_effects=True, vmem_limit_bytes=62 * 1024 * 1024
        ),
    )(child_inverse, child_rhs, child_update, trow, tcol, root_inverse, root_rhs)


def solution(mesh):
    return jax.shard_map(
        functools.partial(per_device, mesh.shape["bulk"], mesh.shape["row"]),
        mesh=mesh,
        in_specs=(
            P(None, "row", "bulk"),
            P(None, "bulk", None),
            P(None, "bulk", "row"),
            P(),
            P("row", "bulk"),
            P("bulk", None),
        ),
        out_specs=(P("bulk", None), P(None, "bulk", None)),
        check_vma=False,
    )
```

```python
import functools

import jax
import jax.numpy as jnp
from jax import lax
from jax.experimental import pallas as pl
from jax.experimental.pallas import tpu as pltpu
from jax.sharding import PartitionSpec as P

MESH = pl.DeviceIdType.MESH
CHUNKS = 2
OFFSET = 1
GROUP = 1
PIECES = 4
f32, bf16 = jnp.float32, jnp.bfloat16


def split(x):
    high = x.astype(bf16)
    return high, (x - high.astype(f32)).astype(bf16)


def bit_orders(bits):
    rest = list(range(1, bits))
    if GROUP == 1:
        return ([(0,)] + [(b,) for b in rest], [(0,)] + [(b,) for b in rest[::-1]])
    groups = [(0,)] + [tuple(rest[i:i + GROUP]) for i in range(0, len(rest), GROUP)]
    return (groups, groups)


def block_position(block, order):
    position = 0
    for group in order:
        for bit in group:
            position = position * 2 + (block // (1 << bit)) % 2
    return position


def dot(a, b):
    return jnp.dot(a, b, preferred_element_type=f32)


def kernel(
    nb, nr, dims,
    ci_hbm, crhs_ref, cu_hbm, trow_ref, tcol_ref, ri_hbm, rrhs_ref,
    root_out, child_out,
    ci, cu, ri,
    part, fcr, fc, ug, frp, frr, fr, rep, repr_, cp, cpr,
    up, upx, bk, bkx, cb, cbx,
    rhs_w, tmp_t,
    load_sem, ar_s, ar_r, ch_s, ch_r,
):
    orders = bit_orders(nb.bit_length() - 1)
    me = lax.axis_index("bulk")
    row = lax.axis_index("row")
    C = fc.shape[-1]
    cols_a, cols_b, own, rows_a, nl = dims

    loads = [
        pltpu.make_async_copy(ci_hbm, ci, load_sem.at[0]),
        pltpu.make_async_copy(cu_hbm, cu, load_sem.at[1]),
        pltpu.make_async_copy(ri_hbm, ri, load_sem.at[2]),
    ]
    for load in loads:
        load.start()

    def bit_of(bit):
        return (me // (1 << bit)) % 2

    def peers(group, part):
        here = 0
        for bit in group:
            here = here * 2 + bit_of(bit)
        found = []
        for mask in range(1, 1 << len(group)):
            index, there = me, 0
            for k, bit in enumerate(group):
                mine = bit_of(bit)
                if (mask >> k) & 1:
                    index = index + (1 << bit) * (1 - 2 * mine)
                    mine = 1 - mine
                there = there * 2 + mine
            found.append((index, there * part))
        return here * part, found

    right = lax.rem(row + 1, nr)
    left = lax.rem(row + nr - 1, nr)
    barrier = pltpu.get_barrier_semaphore()
    greeted = 0
    for group in orders[0]:
        for index, _ in peers(group, 1)[1]:
            pl.semaphore_signal(barrier, inc=1, device_id={"bulk": index}, device_id_type=MESH)
            greeted += 1

    for side in (left, right):
        pl.semaphore_signal(barrier, inc=1, device_id={"row": side}, device_id_type=MESH)
    pl.semaphore_wait(barrier, greeted + 2)

    def remote(src, dst, send, recv, **where):
        return pltpu.make_async_remote_copy(
            src_ref=src, dst_ref=dst, send_sem=send, recv_sem=recv, device_id=where, device_id_type=MESH
        )

    pending = [[] for _ in range(CHUNKS)]

    def flush(h):
        for finish in pending[h]:
            finish()
        pending[h] = []

    def reduce_scatter(h, which, buf, rbuf, starts, out, produce):
        length, off, sends = buf.shape[2], 0, []
        for step in range(len(orders[0])):
            flights = []
            for f in range(2):
                if step == 0:
                    produce(f)
                group = orders[f][step]
                part = length >> len(group)
                here, others = peers(group, part)
                arrivals = []
                for m, (index, there) in enumerate(others):
                    copy = remote(
                        buf.at[h, f, pl.ds(pl.multiple_of(starts[f] + there, part), part)],
                        rbuf.at[h, f, pl.ds(off + m * part, part)],
                        ar_s.at[h, which, f, step, m], ar_r.at[h, which, f, step, m], bulk=index,
                    )
                    copy.start()
                    arrivals.append((copy, off + m * part))
                flights.append((pl.multiple_of(starts[f] + here, part), part, arrivals))
            yield
            if step == 0:
                flush(h)
            for f, (keep, part, arrivals) in enumerate(flights):
                total = buf[h, f, pl.ds(keep, part)]
                for copy, at in arrivals:
                    copy.wait_recv()
                    total = total + rbuf[h, f, pl.ds(at, part)]
                    sends.append(copy.wait_send)
                target = out if step == len(orders[0]) - 1 else buf
                target[h, f, pl.ds(keep, part)] = total
                starts[f] = keep
            off += length - part
            length = part
        pending[h] += sends

    def all_gather(h, which, buf, starts):
        sends, length = [], buf.shape[2] // nb
        for step in reversed(range(len(orders[0]))):
            flights = []
            for f in range(2):
                group = orders[f][step]
                here, others = peers(group, length)
                at = buf.at[h, f, pl.ds(pl.multiple_of(starts[f], length), length)]
                for m, (index, _) in enumerate(others):
                    copy = remote(at, at, ar_s.at[h, which, f, step, m], ar_r.at[h, which, f, step, m], bulk=index)
                    copy.start()
                    flights.append(copy)
                starts[f] = starts[f] - here
            yield
            if not sends:
                flush(h)
            for copy in flights:
                copy.wait_recv()
                sends.append(copy.wait_send)
            length = length << len(group)
        pending[h] += sends

    def chain(h, which, p, x, produce=None, stride=1):
        pieces = p.shape[1]

        @pl.when(row == 0)
        def _():
            x[h, 0] = jnp.zeros(x.shape[2:], f32)

        @pl.when(row == nr - 1)
        def _():
            x[h, 1] = jnp.zeros(x.shape[2:], f32)

        def flow(side, i, has_source, has_target, target):
            copy = remote(
                x.at[h, 2 + side, i], x.at[h, side, i],
                ch_s.at[h, which, side, i], ch_r.at[h, which, side, i], row=target,
            )

            @pl.when(has_source)
            def _():
                copy.wait_recv()

            @pl.when(has_target)
            def _():
                x[h, 2 + side, i] = x[h, side, i] + p[h, i]
                copy.start()

        for t in range(pieces + nr - 1):
            if t > 0:
                yield
            if t == 1:
                flush(h)
            if produce is not None and t < pieces and t % stride == 0:
                produce(t // stride)
            i = t - row

            @pl.when((i >= 0) & (i < pieces))
            def _():
                flow(0, i, row > 0, row < nr - 1, right)

            k = t - (nr - 1 - row)

            @pl.when((k >= 0) & (k < pieces))
            def _():
                flow(1, k, row < nr - 1, row > 0, left)

        def finish():
            for i in range(pieces):
                for side, has_target, target in ((0, row < nr - 1, right), (1, row > 0, left)):
                    @pl.when(has_target)
                    def _():
                        remote(
                            x.at[h, 2 + side, i], x.at[h, side, i],
                            ch_s.at[h, which, side, i], ch_r.at[h, which, side, i], row=target,
                        ).wait_send()

        pending[h].append(finish)

    def times(a_tile, count, store, h, width):
        def body(i, carry):
            high, low = split(a_tile(i))
            both = dot(high, rhs_w[h, :width]) + dot(low, rhs_w[h, :width])
            store(i, both[:, :C] + both[:, C:])
            return carry

        lax.fori_loop(0, count, body, 0)

    def keep_right(h, at, value):
        high, low = split(value)
        rhs_w[h, at, :C] = high
        rhs_w[h, at, C:] = low

    def keep_transposed(h, depth, k_tile, y_tile):
        for k in range(depth // k_tile):
            high, low = split(y_tile(k).T)
            tmp_t[h, :C, k * k_tile:(k + 1) * k_tile] = high
            tmp_t[h, C:, k * k_tile:(k + 1) * k_tile] = low

    def transposed_tile(a_tile, depth, k_tile, width, h):
        total = jnp.zeros((2 * C, width), f32)
        for k in range(depth // k_tile):
            high, low = split(a_tile(k))
            y = tmp_t[h, :, k * k_tile:(k + 1) * k_tile]
            total += dot(y, high) + dot(y, low)
        return (total[:C] + total[C:]).T

    def tiles(n, most):
        size = min(n, most)
        return size, n // size

    def program(h):
        lanes = slice(h * C, (h + 1) * C)
        if h == 0:
            loads[0].wait()
        tm, count = tiles(cols_a, 256)
        def produce1(j):
            keep_right(h, slice(0, cols_b), crhs_ref[j, :, lanes])

            def store(i, value):
                part[h, j, pl.ds(pl.multiple_of(i * tm, tm), tm)] = value

            times(lambda i: ci[j, pl.ds(pl.multiple_of(i * tm, tm), tm), :], count, store, h, cols_b)

        starts = [0, 0]
        yield from reduce_scatter(h, 0, part, fcr, starts, fc, produce1)
        yield from all_gather(h, 1, fc, starts)
        if h == 0:
            loads[1].wait()
        for j in range(2):
            keep_right(h, slice(0, cols_a), fc[h, j])

            def store(i, value, j=j):
                up[h, j] = value

            times(lambda i, j=j: cu[j], 1, store, h, cols_a)
        yield from chain(h, 0, up, upx)
        starts = []
        for j in range(2):
            position = block_position(me, orders[j])
            start = pl.multiple_of(position * nl, nl)
            starts.append(start)
            ug[h, j, pl.ds(start, nl)] = upx[h, 0, j] + up[h, j] + upx[h, 1, j]
        yield from all_gather(h, 2, ug, starts)
        tm, count = tiles(own, 256)
        nu = nb * nl
        kt, kcount = tiles(nu, 512)

        def assemble(i, carry):
            ids = lax.broadcasted_iota(jnp.int32, (tm, kt), 0) + (me * own + i * tm)
            at = pl.ds(pl.multiple_of(i * tm, tm), tm)
            total = jnp.zeros((tm, C), f32)
            for j in range(2):
                for k in range(kcount):
                    ks = slice(k * kt, (k + 1) * kt)
                    hit = jnp.where(ids == trow_ref[j:j + 1, ks], 1.0, 0.0).astype(bf16)
                    high, low = split(ug[h, j, ks])
                    total += dot(hit, high) + dot(hit, low)
            value = rrhs_ref[at, lanes] - total
            high, low = split(value)
            rhs_w[h, at, :C] = high
            rhs_w[h, at, C:] = low
            return carry

        lax.fori_loop(0, count, assemble, 0)
        if h == 0:
            loads[2].wait()
        per = rows_a // 2
        tm4, count4 = tiles(per, 256)

        def produce4(f):
            def store(i, value):
                frp[h, f, pl.ds(pl.multiple_of(i * tm4, tm4), tm4)] = value

            times(
                lambda i: ri[pl.ds(pl.multiple_of(f * per + i * tm4, tm4), tm4), :],
                count4, store, h, own,
            )

        starts = [0, 0]
        yield from reduce_scatter(h, 3, frp, frr, starts, fr, produce4)
        yield from all_gather(h, 4, fr, starts)
        pieces, size = bk.shape[1], bk.shape[2]
        width = min(256, own)
        kt5, _ = tiles(per, 512)
        halves = per // kt5

        keep_transposed(h, rows_a, kt5, lambda k: fr[h, k // halves, (k % halves) * kt5:(k % halves + 1) * kt5])

        def produce5(i):
            value = transposed_tile(
                lambda k: ri[k * kt5:(k + 1) * kt5, i * width:(i + 1) * width], rows_a, kt5, width, h
            )
            for n in range(width // size):
                bk[h, i * (width // size) + n] = value[n * size:(n + 1) * size]

        yield from chain(h, 1, bk, bkx, produce5, width // size)
        for i in range(pieces):
            value = bkx[h, 0, i] + bk[h, i] + bkx[h, 1, i]
            root_out[i * size:(i + 1) * size, lanes] = value
            keep_right(h, slice(i * size, (i + 1) * size), value)
        tm6, count6 = tiles(nu, 256)

        def produce6(j):
            def fetch(i, carry):
                at = pl.ds(pl.multiple_of(i * tm6, tm6), tm6)
                ids = lax.broadcasted_iota(jnp.int32, (tm6, own), 1) + me * own
                hit = jnp.where(ids == tcol_ref[j, at], 1.0, 0.0).astype(bf16)
                both = dot(hit, rhs_w[h, :own])
                rep[h, j, at] = both[:, :C] + both[:, C:]
                return carry

            lax.fori_loop(0, count6, fetch, 0)

        starts = [0, 0]
        yield from reduce_scatter(h, 5, rep, repr_, starts, rep, produce6)
        w7, count7 = tiles(cols_a, 256)

        def produce7(j):
            keep_transposed(h, nl, nl, lambda k: rep[h, j, pl.ds(starts[j], nl)])

            def body(i, carry):
                at = pl.ds(pl.multiple_of(i * w7, w7), w7)
                cp[h, j, at] = transposed_tile(lambda k: cu[j, :, at], nl, nl, w7, h)
                return carry

            lax.fori_loop(0, count7, body, 0)

        starts7 = [0, 0]
        yield from reduce_scatter(h, 6, cp, cpr, starts7, part, produce7)
        yield from all_gather(h, 7, part, starts7)
        pieces8, size8 = cb.shape[1], cb.shape[2]
        w8, count8 = tiles(cols_b, 256)
        kt8, _ = tiles(cols_a, 512)

        def produce8(n):
            j, i = n // count8, n % count8
            if i == 0:
                keep_transposed(
                    h, cols_a, kt8,
                    lambda k: fc[h, j, k * kt8:(k + 1) * kt8] - part[h, j, k * kt8:(k + 1) * kt8],
                )
            value = transposed_tile(
                lambda k: ci[j, k * kt8:(k + 1) * kt8, i * w8:(i + 1) * w8], cols_a, kt8, w8, h
            )
            for m in range(w8 // size8):
                cb[h, n * (w8 // size8) + m] = value[m * size8:(m + 1) * size8]

        yield from chain(h, 2, cb, cbx, produce8, w8 // size8)
        for i in range(pieces8):
            j, k = i // (pieces8 // 2), i % (pieces8 // 2)
            child_out[j, k * size8:(k + 1) * size8, lanes] = cbx[h, 0, i] + cb[h, i] + cbx[h, 1, i]

    running = [program(h) for h in range(CHUNKS)]
    turn = 0
    while any(p is not None for p in running):
        for h in range(CHUNKS):
            if running[h] is not None and turn >= h * OFFSET:
                try:
                    next(running[h])
                except StopIteration:
                    flush(h)
                    running[h] = None
        turn += 1


def per_device(nb, nr, child_inverse, child_rhs, child_update, targets, root_inverse, root_rhs):
    orders = bit_orders(nb.bit_length() - 1)
    _, cols_a, cols_b = child_inverse.shape
    nl = child_update.shape[1]
    rows_a, own = root_inverse.shape
    R = root_rhs.shape[1]
    H, C = CHUNKS, R // CHUNKS
    nu = nb * nl
    blocks = targets.reshape(2, nb, nl)
    placed = []
    for j in range(2):
        source = [0] * nb
        for block in range(nb):
            source[block_position(block, orders[j])] = block
        placed.append(jnp.concatenate([blocks[j, s] for s in source]))
    trow = jnp.stack(placed)
    tcol = trow[:, :, None]
    root_pieces = min(PIECES, own // 32)
    child_pieces = 2 * min(PIECES // 2, cols_b // 32)
    most = max(root_pieces, child_pieces, 2)
    any_, vmem = pl.BlockSpec(memory_space=pl.ANY), pl.BlockSpec(memory_space=pltpu.VMEM)

    def sums(n, count=2):
        return [pltpu.VMEM((H, 2, n, C), f32)] * count

    def chains(pieces, rows):
        return [pltpu.VMEM((H, pieces, rows, C), f32), pltpu.VMEM((H, 4, pieces, rows, C), f32)]

    return pl.pallas_call(
        functools.partial(kernel, nb, nr, (cols_a, cols_b, own, rows_a, nl)),
        out_shape=(
            jax.ShapeDtypeStruct(root_rhs.shape, f32),
            jax.ShapeDtypeStruct(child_rhs.shape, f32),
        ),
        in_specs=[any_, vmem, any_, vmem, vmem, any_, vmem],
        out_specs=(vmem, vmem),
        scratch_shapes=[
            pltpu.VMEM(child_inverse.shape, f32),
            pltpu.VMEM(child_update.shape, f32),
            pltpu.VMEM(root_inverse.shape, f32),
            *sums(cols_a, 3),
            pltpu.VMEM((H, 2, nu, C), f32),
            *sums(rows_a // 2, 3),
            *sums(nu),
            *sums(cols_a),
            *chains(2, nl),
            *chains(root_pieces, own // root_pieces),
            *chains(child_pieces, 2 * cols_b // child_pieces),
            pltpu.VMEM((H, max(own, cols_a, cols_b), 2 * C), bf16),
            pltpu.VMEM((H, 2 * C, max(rows_a, cols_a, nl)), bf16),
            pltpu.SemaphoreType.DMA((3,)),
            pltpu.SemaphoreType.DMA((H, 8, 2, len(orders[0]), (1 << GROUP) - 1)),
            pltpu.SemaphoreType.DMA((H, 8, 2, len(orders[0]), (1 << GROUP) - 1)),
            pltpu.SemaphoreType.DMA((H, 3, 2, most)),
            pltpu.SemaphoreType.DMA((H, 3, 2, most)),
        ],
        compiler_params=pltpu.CompilerParams(
            collective_id=0, has_side_effects=True, vmem_limit_bytes=62 * 1024 * 1024
        ),
    )(child_inverse, child_rhs, child_update, trow, tcol, root_inverse, root_rhs)


def solution(mesh):
    return jax.shard_map(
        functools.partial(per_device, mesh.shape["bulk"], mesh.shape["row"]),
        mesh=mesh,
        in_specs=(
            P(None, "row", "bulk"),
            P(None, "bulk", None),
            P(None, "bulk", "row"),
            P(),
            P("row", "bulk"),
            P("bulk", None),
        ),
        out_specs=(P("bulk", None), P(None, "bulk", None)),
        check_vma=False,
    )
```
